32 devices in a mesh: gen: 4 (over y, core), rows: 4 (over z), img: 2 (over x).
Axes of the slice: x: 2, y: 2, z: 4, core: 2. Of those that a mesh axis runs over, the one named last changes fastest.
Arguments:
- center: bfloat16 [2, 32, 32, 128], P('img', 'rows'), may hold values from -6 to 6
- gens: bfloat16 [2, 256, 32, 32, 128], P('img', 'gen', 'rows'), may hold values from -6 to 6
- weight: bfloat16 [3, 3, 128, 128], replicated, may hold values from -0.1875 to 0.1875
- bias: float32 [128], replicated, may hold values from -3 to 3
- radius: float32 [2, 32, 32, 128], P('img', 'rows'), may hold values from 1 to 4
- state: int32 [2, 32, 32, 128], P('img', 'rows'), may hold values from 0 to 2, as said below
- unstable: int32 [2, 16384], P('img'), may hold values from 0 to 131071, as said below
- d_center: float32 [2, 32, 32, 128], P('img', 'rows'), may hold values from -6 to 6
- d_gens: bfloat16 [2, 256, 32, 32, 128], P('img', 'gen', 'rows'), may hold values from -6 to 6
- d_new: float32 [2, 16384], P('img'), may hold values from -6 to 6
Outputs:
- grad_center: bfloat16 [2, 32, 32, 128], P('img', 'rows')
- grad_gens: bfloat16 [2, 256, 32, 32, 128], P('img', 'gen', 'rows')
- grad_weight: float32 [3, 3, 128, 128], replicated
- grad_bias: float32 [128], replicated
- grad_radius: float32 [2, 16384], P('img', 'rows')
The draws below stay inside these ranges and needn't reach their ends.
Inputs may be any that keep to these rules, and one draw needn't show every extreme that they name: `unstable`: each row lists 16384 different neurons of its image; 0 and the last neuron are always listed. `state`: 2 exactly at the neurons that the image's row of unstable lists, else 0 or 1.
All inputs are finite; a program needn't handle non-finite values.
Results may differ from the reference program's by a relative error of at most 0.0049.
Values may be sent and summed in bfloat16 or wider, within the bound.
A program may use at most 128 MiB of HBM per device.

```python
import math
import jax
import jax.numpy as jnp
from jax import lax

CH = 128
HEIGHT = 32
WIDTH = 32
UNST = 16384
GENS = 256
IMAGES = 2


def unstable_cells(key, image):
    inner_key = jax.random.fold_in(jax.random.fold_in(key, 7331), image)
    cells = HEIGHT * WIDTH * CH
    inner = jax.random.permutation(jax.random.fold_in(inner_key, 1), cells - 2)[:UNST - 2].astype(jnp.int32) + 1
    ends = jnp.array([0, cells - 1], jnp.int32)
    listed = jnp.concatenate([inner, ends])
    order = jax.random.permutation(jax.random.fold_in(inner_key, 2), UNST)
    return listed[order]


def draw_unstable(key, part):
    return jnp.stack([unstable_cells(key, image) for image in range(IMAGES)]).astype(jnp.int32)


def draw_state(key, part):
    planes = []
    for image in range(IMAGES):
        base = jax.random.randint(jax.random.fold_in(jax.random.fold_in(key, 911), image), (HEIGHT * WIDTH * CH,), 0, 2).astype(jnp.int32)
        base = base.at[unstable_cells(key, image)].set(2)
        planes.append(base.reshape(HEIGHT, WIDTH, CH))
    return jnp.stack(planes).astype(jnp.int32)


def steps_of(own_key, extent, split, low, top_value):
    def one(dim, shards_of):
        steps = jax.random.uniform(jax.random.fold_in(jax.random.fold_in(own_key, 6), dim), (shards_of,), jnp.float32, low / len(split), top_value / len(split))
        return jnp.repeat(jnp.exp(steps), extent[dim] // shards_of).reshape((-1,) + (1,) * (len(extent) - dim - 1))

    level = one(*split[0])
    for cut in split[1:]:
        level = level * one(*cut)
    return level


def noise(key, extent, scale, most, cuts=(), kind=jnp.bfloat16):
    entries = scale * jax.random.normal(key, extent, jnp.float32)
    if cuts:
        entries = entries * steps_of(key, extent, cuts, -0.22, 0.18)
    return jnp.clip(entries, -most, most).astype(kind)


def setup_inputs(seed: int = 0) -> dict:
    splits = jax.random.split(jax.random.key(seed), 11)
    center = noise(splits[0], (IMAGES, HEIGHT, WIDTH, CH), 1.0, 6.0, ((0, 2), (1, 4)))
    gens = noise(splits[1], (IMAGES, GENS, HEIGHT, WIDTH, CH), 1.0, 6.0, ((0, 2), (1, 4), (2, 4)))
    weight = noise(splits[2], (3, 3, CH, CH), (9 * CH) ** -0.5, 0.1875)
    bias = noise(splits[3], (CH,), 0.5, 3.0, (), jnp.float32)
    radius = jnp.clip(jnp.exp(math.log(4.0) - 1.3862944 * jax.random.uniform(splits[4], (IMAGES, HEIGHT, WIDTH, CH), jnp.float32) ** steps_of(splits[4], (IMAGES, HEIGHT, WIDTH, CH), ((0, 2), (1, 4)), -0.2, 0.2)), 1.0, 4.0)
    state = draw_state(jax.random.fold_in(splits[10], 71), 0)
    unstable = draw_unstable(jax.random.fold_in(splits[10], 71), 0)
    d_center = noise(splits[7], (IMAGES, HEIGHT, WIDTH, CH), 1.0, 6.0, ((0, 2), (1, 4)), jnp.float32)
    d_gens = noise(splits[8], (IMAGES, GENS, HEIGHT, WIDTH, CH), 1.0, 6.0, ((0, 2), (1, 4), (2, 4)))
    d_new = noise(splits[9], (IMAGES, UNST), 1.0, 6.0, ((0, 2),), jnp.float32)
    return {"center": center, "gens": gens, "weight": weight, "bias": bias, "radius": radius, "state": state, "unstable": unstable, "d_center": d_center, "d_gens": d_gens, "d_new": d_new}


DIMS = ("NHWC", "HWIO", "NHWC")


def conv_same(field, kernel):
    return lax.conv_general_dilated(field, kernel, (1, 1), ((1, 1), (1, 1)), dimension_numbers=DIMS, preferred_element_type=jnp.float32)


def relu_terms(y_center, products, radius, state, d_center, extra):
    unstable_mask = state == 2
    safe_r = jnp.where(unstable_mask, radius, 1.0)
    two_r = 2.0 * safe_r
    slope = jnp.where(unstable_mask, (y_center + safe_r) / two_r, jnp.where(state == 1, 1.0, 0.0))
    d_mu = d_center + extra
    d_lam = d_center * y_center + products
    d_yc = slope * d_center + jnp.where(unstable_mask, (d_lam - d_mu * y_center) / two_r, 0.0)
    d_rad = jnp.where(unstable_mask, -d_lam * y_center / (two_r * safe_r) + d_mu * (0.25 + y_center * y_center / (two_r * two_r)), 0.0)
    return slope, d_yc, d_rad


def reference(center, gens, weight, bias, radius, state, unstable, d_center, d_gens, d_new):
    flipped = jnp.transpose(weight[::-1, ::-1], (0, 1, 3, 2))
    cells = HEIGHT * WIDTH * CH
    grad_w = jnp.zeros((3, 3, CH, CH), jnp.float32)
    grad_b = jnp.zeros((CH,), jnp.float32)
    centers_out = []
    gens_out = []
    lists_out = []
    for image in range(IMAGES):
        stacked = jnp.concatenate([center[image][None], gens[image]], axis=0)
        forward = conv_same(stacked, weight)
        y_center = forward[0] + bias
        products = jnp.sum(d_gens[image].astype(jnp.float32) * forward[1:], axis=0)
        extra = jnp.zeros((cells,), jnp.float32).at[unstable[image]].add(d_new[image]).reshape(HEIGHT, WIDTH, CH)
        slope, d_yc, d_rad = relu_terms(y_center, products, radius[image], state[image], d_center[image], extra)
        d_all = jnp.concatenate([d_yc.astype(jnp.bfloat16)[None], (slope * d_gens[image].astype(jnp.float32)).astype(jnp.bfloat16)], axis=0)
        backward = conv_same(d_all, flipped).astype(jnp.bfloat16)
        centers_out.append(backward[0])
        gens_out.append(backward[1:])
        padded = jnp.pad(stacked, ((0, 0), (1, 1), (1, 1), (0, 0)))
        flat_d = d_all.reshape(-1, CH)
        taps = []
        for row_off in range(3):
            for col_off in range(3):
                window = padded[:, row_off:row_off + HEIGHT, col_off:col_off + WIDTH, :].reshape(-1, CH)
                taps.append(jnp.dot(window.T, flat_d, preferred_element_type=jnp.float32))
        grad_w = grad_w + jnp.stack(taps).reshape(3, 3, CH, CH)
        grad_b = grad_b + jnp.sum(d_yc, axis=(0, 1))
        lists_out.append(d_rad.reshape(-1)[unstable[image]])
    positions = float(IMAGES * HEIGHT * WIDTH)
    return (jnp.stack(centers_out), jnp.stack(gens_out), grad_w / positions, grad_b / positions, jnp.stack(lists_out))
```

```python
import functools

import jax
import jax.numpy as jnp
from jax import lax
from jax.experimental import pallas as pl
from jax.experimental.pallas import tpu as pltpu
from jax.sharding import PartitionSpec as P

DIMS = ("NHWC", "HWIO", "NHWC")
F32 = jnp.float32
BF16 = jnp.bfloat16


def edges(array, dim, axis):
    n, length = lax.axis_size(axis), array.shape[dim]
    up = [(i, i + 1) for i in range(n - 1)]
    down = [(i + 1, i) for i in range(n - 1)]
    last = lax.slice_in_dim(array, length - 1, length, axis=dim)
    first = lax.slice_in_dim(array, 0, 1, axis=dim)
    return lax.ppermute(last, axis, up), lax.ppermute(first, axis, down)


def power_of_two(n):
    return n & (n - 1) == 0


def sum_over(value, axis):
    n = lax.axis_size(axis)
    if not power_of_two(n):
        return lax.psum(value, axis)
    bit = 1
    while bit < n:
        value = value + lax.ppermute(value, axis, [(i, i ^ bit) for i in range(n)])
        bit *= 2
    return value


def block_of(array, index, size):
    return lax.dynamic_slice_in_dim(array, index * size, size, 0)


def scatter_sum(chunk, axis):
    n, me = lax.axis_size(axis), lax.axis_index(axis)
    size = chunk.shape[0] // n
    total = block_of(chunk, me, size)
    for k in range(1, n):
        part = block_of(chunk, (me + k) % n, size)
        total = total + lax.ppermute(part, axis, [(i, (i + k) % n) for i in range(n)])
    return total


def gather_blocks(block, axis):
    n, me = lax.axis_size(axis), lax.axis_index(axis)
    size = block.shape[0]
    out = jnp.zeros((n * size,) + block.shape[1:], block.dtype)
    out = lax.dynamic_update_slice_in_dim(out, block, me * size, 0)
    for k in range(1, n):
        part = lax.ppermute(block, axis, [(i, (i + k) % n) for i in range(n)])
        out = lax.dynamic_update_slice_in_dim(out, part, ((me - k) % n) * size, 0)
    return out


def halve(chunk, late, axis):
    n, me = lax.axis_size(axis), lax.axis_index(axis)
    bit = 1
    while bit < n:
        half = chunk.shape[0] // 2
        mine = (me // bit) % 2
        part = block_of(chunk, 1 - mine, half)
        got = lax.ppermute(part, axis, [(i, i ^ bit) for i in range(n)])
        chunk = block_of(chunk, mine, half) + got
        if late is not None:
            late = block_of(late, mine, half)
        bit *= 2
    return chunk, late


def double(chunk, axis):
    n, me = lax.axis_size(axis), lax.axis_index(axis)
    bit = n // 2
    while bit >= 1:
        mine = (me // bit) % 2
        got = lax.ppermute(chunk, axis, [(i, i ^ bit) for i in range(n)])
        low = jnp.where(mine == 0, chunk, got)
        high = jnp.where(mine == 0, got, chunk)
        chunk = jnp.concatenate([low, high], axis=0)
        bit //= 2
    return chunk


def total_over_mesh(local, late):
    sizes = [lax.axis_size(a) for a in ("gen", "img", "rows")]
    if not all(power_of_two(s) for s in sizes):
        return lax.psum(lax.psum(local, "gen") + late, ("rows", "img"))
    chunk, late = halve(local, late, "gen")
    chunk = chunk + late
    chunk, _ = halve(chunk, None, "img")
    chunk = scatter_sum(chunk, "rows")
    chunk = gather_blocks(chunk, "rows")
    return double(double(chunk, "img"), "gen")


def row_pairs(rows):
    pairs = (len(rows) - 2) // 2
    c = rows[0].shape[-1]
    flat = [r.reshape(-1, c) for r in rows]
    return jnp.concatenate(
        [jnp.concatenate([flat[2 * p + i] for i in range(4)], axis=1) for p in range(pairs)],
        axis=0,
    )


def band_rows(x_ref, top_ref, bottom_ref):
    band = x_ref.shape[1]
    return [top_ref[...]] + [x_ref[:, h] for h in range(band)] + [bottom_ref[...]]


def column(count, width):
    return lax.broadcasted_iota(jnp.int32, (count, 1), 0) % width


def to_right(v, col):
    return jnp.where(col == 0, 0.0, pltpu.roll(v, 1, 0))


def to_left(v, col, width):
    return jnp.where(col == width - 1, 0.0, pltpu.roll(v, v.shape[0] - 1, 0))


def conv_pairs(lhs, w_ref, r, width, c, col):
    span = 3 * c
    taps = jnp.dot(lhs, w_ref[:, r * span : (r + 1) * span], preferred_element_type=F32)
    return (
        to_right(taps[:, :c], col)
        + taps[:, c : 2 * c]
        + to_left(taps[:, 2 * c :], col, width)
    )


def products_kernel(x_ref, top_ref, bottom_ref, d_ref, w_ref, out_ref):
    @pl.when(pl.program_id(0) == 0)
    def _():
        out_ref[...] = jnp.zeros_like(out_ref)

    g, band, width, c = x_ref.shape
    lhs = row_pairs(band_rows(x_ref, top_ref, bottom_ref))
    col = column(lhs.shape[0], width)
    for r in range(2):
        y = conv_pairs(lhs, w_ref, r, width, c, col).reshape(band // 2, g, width, c)
        for p in range(band // 2):
            h = 2 * p + r
            out_ref[h] += jnp.sum(d_ref[:, h].astype(F32) * y[p], axis=0)


def wgrad_kernel(x_ref, top_ref, bottom_ref, d_ref, slope_ref, out_ref):
    @pl.when(pl.program_id(0) == 0)
    def _():
        out_ref[...] = jnp.zeros_like(out_ref)

    g, band, width, c = x_ref.shape
    lhs = row_pairs(band_rows(x_ref, top_ref, bottom_ref))
    col = column(lhs.shape[0], width)
    parts = []
    for r in range(2):
        d = jnp.concatenate(
            [
                (slope_ref[h][None] * d_ref[:, h].astype(F32)).reshape(-1, c)
                for h in range(r, band, 2)
            ],
            axis=0,
        )
        parts += [
            to_left(d, col, width).astype(BF16),
            d.astype(BF16),
            to_right(d, col).astype(BF16),
        ]
    rhs = jnp.concatenate(parts, axis=1)
    out_ref[...] += lax.dot_general(
        lhs, rhs, (((0,), (0,)), ((), ())), preferred_element_type=F32
    )


def backward_kernel(d_ref, top_ref, bottom_ref, slope_ref, w_ref, *refs):
    out_ref = refs[-1]
    g, band, width, c = d_ref.shape
    rows = [
        (slope_ref[j][None] * row.astype(F32)).astype(BF16)
        for j, row in enumerate(band_rows(d_ref, top_ref, bottom_ref))
    ]
    lhs = row_pairs(rows)
    col = column(lhs.shape[0], width)
    for r in range(2):
        y = conv_pairs(lhs, w_ref, r, width, c, col).reshape(band // 2, g, width, c)
        for p in range(band // 2):
            out_ref[:, 2 * p + r] = y[p].astype(BF16)


def spread_kernel(place_ref, chan_ref, value_ref, out_ref):
    @pl.when(pl.program_id(0) == 0)
    def _():
        out_ref[...] = jnp.zeros_like(out_ref)

    places, c = out_ref.shape
    count = place_ref.shape[1]
    at_place = lax.broadcasted_iota(jnp.int32, (places, count), 0) == place_ref[...]
    at_chan = lax.broadcasted_iota(jnp.int32, (c, count), 0) == chan_ref[...]
    value = value_ref[...]
    high = value.astype(BF16).astype(F32)
    mid = (value - high).astype(BF16).astype(F32)
    low = value - high - mid
    terms = jnp.concatenate(
        [jnp.where(at_chan, part, 0.0).astype(BF16) for part in (high, mid, low)], axis=0
    )
    hit = jnp.where(at_place, 1.0, 0.0).astype(BF16)
    both = lax.dot_general(hit, terms, (((1,), (1,)), ((), ())), preferred_element_type=F32)
    out_ref[...] += both[:, :c] + both[:, c : 2 * c] + both[:, 2 * c :]


def pick_kernel(place_ref, chan_ref, field_ref, out_ref):
    places = field_ref.shape[1]
    c = field_ref.shape[0] // 3
    count = place_ref.shape[1]
    at_place = lax.broadcasted_iota(jnp.int32, (places, count), 0) == place_ref[...]
    at_chan = lax.broadcasted_iota(jnp.int32, (c, count), 0) == chan_ref[...]
    hit = jnp.where(at_place, 1.0, 0.0).astype(BF16)
    got = jnp.dot(field_ref[...], hit, preferred_element_type=F32)
    got = got[:c] + got[c : 2 * c] + got[2 * c :]
    out_ref[...] = jnp.sum(jnp.where(at_chan, got, 0.0), axis=0, keepdims=True)


def group_of(count, most):
    g = min(count, most)
    while count % g:
        g -= 1
    return g


def gen_spec(g, shape, first=0):
    zeros = (0,) * (len(shape) - 1)
    return pl.BlockSpec((g,) + tuple(shape[1:]), lambda i: (i + first,) + zeros)


def whole_spec(shape):
    zeros = (0,) * len(shape)
    return pl.BlockSpec(tuple(shape), lambda i: zeros)


def cost(count, band, width, c):
    return pl.CostEstimate(
        flops=count * band * width * c * c * 24,
        bytes_accessed=count * band * width * c * 4,
        transcendentals=0,
    )


def products_call(x, top, bottom, d, w):
    n, band, width, c = x.shape
    g = group_of(n, 8)
    return pl.pallas_call(
        products_kernel,
        grid=(n // g,),
        in_specs=[
            gen_spec(g, x.shape),
            gen_spec(g, top.shape),
            gen_spec(g, bottom.shape),
            gen_spec(g, d.shape),
            whole_spec(w.shape),
        ],
        out_specs=whole_spec((band, width, c)),
        out_shape=jax.ShapeDtypeStruct((band, width, c), F32),
        cost_estimate=cost(n, band, width, c),
        name="products",
    )(x, top, bottom, d, w)


def wgrad_call(x, top, bottom, d, slope, part, parts):
    n, band, width, c = x.shape
    n //= parts
    g = group_of(n, 8)
    first = part * (n // g)
    return pl.pallas_call(
        wgrad_kernel,
        grid=(n // g,),
        in_specs=[
            gen_spec(g, x.shape, first),
            gen_spec(g, top.shape, first),
            gen_spec(g, bottom.shape, first),
            gen_spec(g, d.shape, first),
            whole_spec(slope.shape),
        ],
        out_specs=whole_spec((4 * c, 6 * c)),
        out_shape=jax.ShapeDtypeStruct((4 * c, 6 * c), F32),
        cost_estimate=cost(n, band, width, c),
        name="wgrad",
    )(x, top, bottom, d, slope)


def backward_call(d, top, bottom, slope, w, out, part, parts):
    n, band, width, c = d.shape
    n //= parts
    g = group_of(n, 8)
    first = part * (n // g)
    args = [d, top, bottom, slope, w]
    specs = [
        gen_spec(g, d.shape, first),
        gen_spec(g, top.shape, first),
        gen_spec(g, bottom.shape, first),
        whole_spec(slope.shape),
        whole_spec(w.shape),
    ]
    aliases = {}
    if out is not None:
        aliases = {len(args): 0}
        args.append(out)
        specs.append(pl.BlockSpec(memory_space=pl.ANY))
    return pl.pallas_call(
        backward_kernel,
        grid=(n // g,),
        in_specs=specs,
        out_specs=gen_spec(g, d.shape, first),
        out_shape=jax.ShapeDtypeStruct(d.shape, BF16),
        input_output_aliases=aliases,
        cost_estimate=cost(n, band, width, c),
        name="backward",
    )(*args)


def list_call(kernel, place, chan, extra, extra_specs, out_shape, out_spec, name, step):
    count = place.shape[1]
    row = lambda: pl.BlockSpec((1, step), lambda i: (0, i))
    return pl.pallas_call(
        kernel,
        grid=(count // step,),
        in_specs=[row(), row()] + extra_specs,
        out_specs=out_spec,
        out_shape=out_shape,
        cost_estimate=pl.CostEstimate(
            flops=count * 256 * 768, bytes_accessed=count * 12, transcendentals=0
        ),
        name=name,
    )(place, chan, extra)


def spread_values(place, chan, values, places, c):
    step = group_of(place.shape[1], 2048)
    return list_call(
        spread_kernel, place, chan, values,
        [pl.BlockSpec((1, step), lambda i: (0, i))],
        jax.ShapeDtypeStruct((places, c), F32),
        whole_spec((places, c)), "spread", step,
    )


def pick_values(place, chan, field):
    step = group_of(place.shape[1], 2048)
    high = field.astype(BF16)
    rest = field - high.astype(F32)
    mid = rest.astype(BF16)
    low = (rest - mid.astype(F32)).astype(BF16)
    split = jnp.concatenate([high, mid, low], axis=1).T
    return list_call(
        pick_kernel, place, chan, split,
        [whole_spec(split.shape)],
        jax.ShapeDtypeStruct((1, place.shape[1]), F32),
        pl.BlockSpec((1, step), lambda i: (0, i)), "pick", step,
    )


def pair_weights(weight):
    c, o = weight.shape[2], weight.shape[3]
    zero = jnp.zeros((c, 3 * o), weight.dtype)
    side = jnp.transpose(weight, (0, 2, 1, 3)).reshape(3 * c, 3 * o)
    return jnp.concatenate(
        [
            jnp.concatenate([side, zero], axis=0),
            jnp.concatenate([zero, side], axis=0),
        ],
        axis=1,
    )


def conv_band(field, kernel):
    return lax.conv_general_dilated(
        field, kernel, (1, 1), ((0, 0), (1, 1)), dimension_numbers=DIMS,
        preferred_element_type=F32,
    )


def relu_terms(y_center, products, radius, state, d_center, extra):
    unstable_mask = state == 2
    safe_r = jnp.where(unstable_mask, radius, 1.0)
    two_r = 2.0 * safe_r
    slope = slope_of(y_center, radius, state)
    d_mu = d_center + extra
    d_lam = d_center * y_center + products
    d_yc = slope * d_center + jnp.where(unstable_mask, (d_lam - d_mu * y_center) / two_r, 0.0)
    d_rad = jnp.where(
        unstable_mask,
        -d_lam * y_center / (two_r * safe_r)
        + d_mu * (0.25 + y_center * y_center / (two_r * two_r)),
        0.0,
    )
    return d_yc, d_rad


def slope_of(y_center, radius, state):
    unstable_mask = state == 2
    safe_r = jnp.where(unstable_mask, radius, 1.0)
    return jnp.where(
        unstable_mask, (y_center + safe_r) / (2.0 * safe_r), jnp.where(state == 1, 1.0, 0.0)
    )


def on_device(center, gens, weight, bias, radius, state, unstable, d_center, d_gens, d_new):
    band, width, c = center.shape[1:]
    row_pos = lax.axis_index("rows")
    flipped = jnp.transpose(weight[::-1, ::-1], (0, 1, 3, 2))
    forward_w = pair_weights(weight)
    backward_w = pair_weights(flipped)
    x, d = gens[0], d_gens[0]

    c_top, c_bottom = edges(center, 1, "rows")
    x_top, x_bottom = (e[:, 0] for e in edges(x, 1, "rows"))
    d_top, d_bottom = (e[:, 0] for e in edges(d, 1, "rows"))

    ids = unstable
    place = ids // c - row_pos * (band * width)
    chan = ids % c
    extra = spread_values(place, chan, d_new, band * width, c).reshape(band, width, c)

    padded = jnp.concatenate([c_top, center, c_bottom], axis=1)
    y_center = conv_band(padded, weight)[0] + bias
    slope = slope_of(y_center, radius[0], state[0])
    s_top, s_bottom = edges(slope, 0, "rows")
    slopes = jnp.concatenate([s_top, slope, s_bottom], axis=0)

    partial_sum = products_call(x, x_top, x_bottom, d, forward_w)
    products = sum_over(partial_sum, "gen")
    taps = wgrad_call(x, x_top, x_bottom, d, slope, 0, 2)
    taps = taps + wgrad_call(x, x_top, x_bottom, d, slope, 1, 2)
    taps = taps.reshape(4, c, 2, 3, c)
    local_w = (taps[:3, :, 0] + taps[1:, :, 1]).transpose(0, 2, 1, 3).reshape(9 * c, c)

    d_yc, d_rad = relu_terms(y_center, products, radius[0], state[0], d_center[0], extra)
    d_yc16 = d_yc.astype(BF16)
    t_top, t_bottom = edges(d_yc16, 0, "rows")
    d_padded = jnp.concatenate([t_top, d_yc16, t_bottom], axis=0)[None]
    grad_center = conv_band(d_padded, flipped).astype(BF16)

    wide = jnp.pad(padded[0], ((0, 0), (1, 1), (0, 0)))
    windows = jnp.concatenate(
        [
            wide[a : a + band, b : b + width].reshape(-1, c)
            for a in range(3)
            for b in range(3)
        ],
        axis=1,
    )
    center_w = lax.dot_general(
        windows, d_yc16.reshape(-1, c), (((0,), (0,)), ((), ())), preferred_element_type=F32
    )
    center_b = jnp.sum(d_yc, axis=(0, 1))[None]
    parts = lax.axis_size("gen") * lax.axis_size("rows") * lax.axis_size("img") * 8
    spare = -(9 * c) % parts or parts
    local = jnp.pad(local_w, ((0, spare), (0, 0)))
    late = jnp.concatenate([center_w, center_b, jnp.zeros((spare - 1, c), F32)], axis=0)
    totals = total_over_mesh(local, late)
    positions = float(band * lax.axis_size("rows") * width * lax.axis_size("img"))
    grad_weight = (totals[: 9 * c] / positions).reshape(3, 3, c, c)
    grad_bias = totals[9 * c] / positions

    out = None
    pieces = 4 if x.shape[0] % 32 == 0 else 1
    for part in range(pieces):
        out = backward_call(d, d_top, d_bottom, slopes, backward_w, out, part, pieces)

    picked = pick_values(place, chan, d_rad.reshape(-1, c))
    block = unstable.shape[1] // lax.axis_size("rows")
    mine = scatter_sum(picked.reshape(-1, 128) if block % 128 == 0 else picked[0], "rows")
    grad_radius = mine.reshape(1, block)
    return (grad_center, out[None], grad_weight, grad_bias, grad_radius)


def solution(mesh):
    return jax.shard_map(
        on_device,
        mesh=mesh,
        in_specs=(
            P("img", "rows", None, None),
            P("img", "gen", "rows", None, None),
            P(),
            P(),
            P("img", "rows", None, None),
            P("img", "rows", None, None),
            P("img", None),
            P("img", "rows", None, None),
            P("img", "gen", "rows", None, None),
            P("img", None),
        ),
        out_specs=(
            P("img", "rows", None, None),
            P("img", "gen", "rows", None, None),
            P(),
            P(),
            P("img", "rows"),
        ),
        check_vma=False,
    )
```

```python
import functools

import jax
import jax.numpy as jnp
from jax import lax
from jax.experimental import pallas as pl
from jax.experimental.pallas import tpu as pltpu
from jax.sharding import PartitionSpec as P

DIMS = ("NHWC", "HWIO", "NHWC")
F32 = jnp.float32
BF16 = jnp.bfloat16


def neighbours(last, first, axis):
    n = lax.axis_size(axis)
    up = [(i, i + 1) for i in range(n - 1)]
    down = [(i + 1, i) for i in range(n - 1)]
    return lax.ppermute(last, axis, up), lax.ppermute(first, axis, down)


def edges(array, axis):
    return neighbours(array[-1:], array[:1], axis)


def no_fill(got, before):
    return got


class Filler:
    def __init__(self, call, operand, pieces, steps):
        self.call, self.operand, self.pieces = call, operand, pieces
        self.steps, self.step, self.done, self.out = steps, 0, 0, None

    def run(self, operand):
        self.out = self.call(operand, self.out, self.done, self.pieces)
        self.done += 1

    def __call__(self, got, before):
        self.step += 1
        if self.step in self.steps and self.done < self.pieces:
            _, operand = lax.optimization_barrier((before, self.operand))
            self.run(operand)
            got, self.out = lax.optimization_barrier((got, self.out))
        return got

    def finish(self):
        while self.done < self.pieces:
            self.run(self.operand)
        return self.out


def power_of_two(n):
    return n & (n - 1) == 0


def sum_over(value, axis, fills):
    n = lax.axis_size(axis)
    if not power_of_two(n):
        return lax.psum(value, axis)
    bit = 1
    while bit < n:
        got = lax.ppermute(value, axis, [(i, i ^ bit) for i in range(n)])
        if fills:
            got = fills.pop(0)(got, value)
        value = value + got
        bit *= 2
    return value


def block_of(array, index, size):
    return lax.dynamic_slice_in_dim(array, index * size, size, 0)


def scatter_sum(chunk, axis):
    n, me = lax.axis_size(axis), lax.axis_index(axis)
    size = chunk.shape[0] // n
    total = block_of(chunk, me, size)
    for k in range(1, n):
        part = block_of(chunk, (me + k) % n, size)
        total = total + lax.ppermute(part, axis, [(i, (i + k) % n) for i in range(n)])
    return total


def gather_blocks(block, axis):
    n, me = lax.axis_size(axis), lax.axis_index(axis)
    size = block.shape[0]
    out = jnp.zeros((n * size,) + block.shape[1:], block.dtype)
    out = lax.dynamic_update_slice_in_dim(out, block, me * size, 0)
    for k in range(1, n):
        part = lax.ppermute(block, axis, [(i, (i + k) % n) for i in range(n)])
        out = lax.dynamic_update_slice_in_dim(out, part, ((me - k) % n) * size, 0)
    return out


def halve(chunk, late, axis, fill):
    n, me = lax.axis_size(axis), lax.axis_index(axis)
    bit = 1
    while bit < n:
        half = chunk.shape[0] // 2
        mine = (me // bit) % 2
        part = block_of(chunk, 1 - mine, half)
        got = lax.ppermute(part, axis, [(i, i ^ bit) for i in range(n)])
        got = fill(got, part)
        chunk = block_of(chunk, mine, half) + got
        if late is not None:
            late = block_of(late, mine, half)
        bit *= 2
    return chunk, late


def double(chunk, axis, fill):
    n, me = lax.axis_size(axis), lax.axis_index(axis)
    bit = n // 2
    while bit >= 1:
        mine = (me // bit) % 2
        got = lax.ppermute(chunk, axis, [(i, i ^ bit) for i in range(n)])
        got = fill(got, chunk)
        low = jnp.where(mine == 0, chunk, got)
        high = jnp.where(mine == 0, got, chunk)
        chunk = jnp.concatenate([low, high], axis=0)
        bit //= 2
    return chunk


def total_over_mesh(local, late, fill):
    sizes = [lax.axis_size(a) for a in ("gen", "img", "rows")]
    if not all(power_of_two(s) for s in sizes):
        return lax.psum(lax.psum(local, "gen") + late, ("rows", "img"))
    chunk, late = halve(local, late, "gen", fill)
    chunk = chunk + late
    chunk, _ = halve(chunk, None, "img", fill)
    chunk = scatter_sum(chunk, "rows")
    chunk = gather_blocks(chunk, "rows")
    return double(double(chunk, "img", fill), "gen", fill)


def row_pairs(rows):
    pairs = (len(rows) - 2) // 2
    c = rows[0].shape[-1]
    flat = [r.reshape(-1, c) for r in rows]
    return jnp.concatenate(
        [jnp.concatenate([flat[2 * p + i] for i in range(4)], axis=1) for p in range(pairs)],
        axis=0,
    )


def band_rows(x_ref, top_ref, bottom_ref):
    band = x_ref.shape[1]
    return [top_ref[...]] + [x_ref[:, h] for h in range(band)] + [bottom_ref[...]]


def column(count, width):
    return lax.broadcasted_iota(jnp.int32, (count, 1), 0) % width


def to_right(v, col):
    return jnp.where(col == 0, 0.0, pltpu.roll(v, 1, 0))


def to_left(v, col, width):
    return jnp.where(col == width - 1, 0.0, pltpu.roll(v, v.shape[0] - 1, 0))


def conv_pairs(lhs, w_ref, r, width, c, col):
    span = 3 * c
    taps = jnp.dot(lhs, w_ref[:, r * span : (r + 1) * span], preferred_element_type=F32)
    return (
        to_right(taps[:, :c], col)
        + taps[:, c : 2 * c]
        + to_left(taps[:, 2 * c :], col, width)
    )


def products_kernel(x_ref, top_ref, bottom_ref, d_ref, w_ref, out_ref):
    @pl.when(pl.program_id(0) == 0)
    def _():
        out_ref[...] = jnp.zeros_like(out_ref)

    g, band, width, c = x_ref.shape
    lhs = row_pairs(band_rows(x_ref, top_ref, bottom_ref))
    col = column(lhs.shape[0], width)
    for r in range(2):
        y = conv_pairs(lhs, w_ref, r, width, c, col).reshape(band // 2, g, width, c)
        for p in range(band // 2):
            h = 2 * p + r
            out_ref[h] += jnp.sum(d_ref[:, h].astype(F32) * y[p], axis=0)


def wgrad_kernel(last, x_ref, top_ref, bottom_ref, d_ref, slope_ref, *refs):
    acc_ref = refs[-1]

    @pl.when(pl.program_id(0) == 0)
    def _():
        acc_ref[...] = refs[0][...] if len(refs) == 3 else jnp.zeros_like(acc_ref)

    g, band, width, c = x_ref.shape
    lhs = row_pairs(band_rows(x_ref, top_ref, bottom_ref))
    col = column(lhs.shape[0], width)
    parts = []
    for r in range(2):
        d = jnp.concatenate(
            [
                (slope_ref[h][None] * d_ref[:, h].astype(F32)).reshape(-1, c)
                for h in range(r, band, 2)
            ],
            axis=0,
        )
        parts += [
            to_left(d, col, width).astype(BF16),
            d.astype(BF16),
            to_right(d, col).astype(BF16),
        ]
    rhs = jnp.concatenate(parts, axis=1)
    acc_ref[...] += lax.dot_general(
        lhs, rhs, (((0,), (0,)), ((), ())), preferred_element_type=F32
    )

    @pl.when(pl.program_id(0) == pl.num_programs(0) - 1)
    def _():
        out_ref = refs[-2]
        if not last:
            out_ref[...] = acc_ref[...]
            return
        for a in range(3):
            for b in range(3):
                first = acc_ref[a * c : (a + 1) * c, b * c : (b + 1) * c]
                second = acc_ref[(a + 1) * c : (a + 2) * c, (3 + b) * c : (4 + b) * c]
                out_ref[(a * 3 + b) * c : (a * 3 + b + 1) * c] = first + second
        spare = out_ref.shape[0] - 9 * c
        out_ref[9 * c :] = jnp.zeros((spare, c), F32)


def backward_kernel(d_ref, top_ref, bottom_ref, slope_ref, w_ref, *refs):
    out_ref = refs[-1]
    g, band, width, c = d_ref.shape
    rows = [
        (slope_ref[j][None] * row.astype(F32)).astype(BF16)
        for j, row in enumerate(band_rows(d_ref, top_ref, bottom_ref))
    ]
    lhs = row_pairs(rows)
    col = column(lhs.shape[0], width)
    for r in range(2):
        y = conv_pairs(lhs, w_ref, r, width, c, col).reshape(band // 2, g, width, c)
        for p in range(band // 2):
            out_ref[:, 2 * p + r] = y[p].astype(BF16)


def spread_kernel(place_ref, chan_ref, value_ref, out_ref):
    @pl.when(pl.program_id(0) == 0)
    def _():
        out_ref[...] = jnp.zeros_like(out_ref)

    places, c = out_ref.shape
    count = place_ref.shape[1]
    at_place = lax.broadcasted_iota(jnp.int32, (places, count), 0) == place_ref[...]
    at_chan = lax.broadcasted_iota(jnp.int32, (c, count), 0) == chan_ref[...]
    value = value_ref[...]
    high = value.astype(BF16).astype(F32)
    low = value - high
    terms = jnp.concatenate(
        [jnp.where(at_chan, part, 0.0).astype(BF16) for part in (high, low)], axis=0
    )
    hit = jnp.where(at_place, 1.0, 0.0).astype(BF16)
    both = lax.dot_general(hit, terms, (((1,), (1,)), ((), ())), preferred_element_type=F32)
    out_ref[...] += both[:, :c] + both[:, c:]


def pick_kernel(place_ref, chan_ref, field_ref, out_ref):
    places = field_ref.shape[1]
    c = field_ref.shape[0] // 2
    count = place_ref.shape[1]
    at_place = lax.broadcasted_iota(jnp.int32, (places, count), 0) == place_ref[...]
    at_chan = lax.broadcasted_iota(jnp.int32, (c, count), 0) == chan_ref[...]
    hit = jnp.where(at_place, 1.0, 0.0).astype(BF16)
    got = jnp.dot(field_ref[...], hit, preferred_element_type=F32)
    got = got[:c] + got[c:]
    out_ref[...] = jnp.sum(jnp.where(at_chan, got, 0.0), axis=0, keepdims=True)


def group_of(count, most):
    g = min(count, most)
    while count % g:
        g -= 1
    return g


def gen_spec(g, shape, first=0):
    zeros = (0,) * (len(shape) - 1)
    return pl.BlockSpec((g,) + tuple(shape[1:]), lambda i: (i + first,) + zeros)


def whole_spec(shape):
    zeros = (0,) * len(shape)
    return pl.BlockSpec(tuple(shape), lambda i: zeros)


def cost(count, band, width, c):
    return pl.CostEstimate(
        flops=count * band * width * c * c * 24,
        bytes_accessed=count * band * width * c * 4,
        transcendentals=0,
    )


def edges_kernel(x_last, d_last, x_first, d_first, last_ref, first_ref):
    n = x_last.shape[0]
    last_ref[:n] = x_last[:, 0]
    last_ref[n:] = d_last[:, 0]
    first_ref[:n] = x_first[:, 0]
    first_ref[n:] = d_first[:, 0]


def edge_rows(x, d):
    n, band, width, c = x.shape
    row = lambda h: pl.BlockSpec((n, 1, width, c), lambda i: (0, h, 0, 0))
    shape = (2 * n, width, c)
    return pl.pallas_call(
        edges_kernel,
        grid=(1,),
        in_specs=[row(band - 1), row(band - 1), row(0), row(0)],
        out_specs=[whole_spec(shape)] * 2,
        out_shape=[jax.ShapeDtypeStruct(shape, BF16)] * 2,
        name="edges",
    )(x, d, x, d)


def products_call(x, top, bottom, d, w):
    n, band, width, c = x.shape
    g = group_of(n, 8)
    return pl.pallas_call(
        products_kernel,
        grid=(n // g,),
        in_specs=[
            gen_spec(g, x.shape),
            gen_spec(g, top.shape),
            gen_spec(g, bottom.shape),
            gen_spec(g, d.shape),
            whole_spec(w.shape),
        ],
        out_specs=whole_spec((band, width, c)),
        out_shape=jax.ShapeDtypeStruct((band, width, c), F32),
        cost_estimate=cost(n, band, width, c),
        name="products",
    )(x, top, bottom, d, w)


def wgrad_call(x, top, bottom, d, slope, acc, part, parts, rows):
    n, band, width, c = x.shape
    n //= parts
    g = group_of(n, 8)
    first = part * (n // g)
    last = part == parts - 1
    shape = (rows, c) if last else (4 * c, 6 * c)
    args = [x, top, bottom, d, slope] + ([] if acc is None else [acc])
    return pl.pallas_call(
        functools.partial(wgrad_kernel, last),
        grid=(n // g,),
        in_specs=[
            gen_spec(g, x.shape, first),
            gen_spec(g, top.shape, first),
            gen_spec(g, bottom.shape, first),
            gen_spec(g, d.shape, first),
        ]
        + [whole_spec(a.shape) for a in args[4:]],
        out_specs=whole_spec(shape),
        out_shape=jax.ShapeDtypeStruct(shape, F32),
        scratch_shapes=[pltpu.VMEM((4 * c, 6 * c), F32)],
        cost_estimate=cost(n, band, width, c),
        name="wgrad",
    )(*args)


def backward_call(d, top, bottom, slope, w, out, part, parts):
    n, band, width, c = d.shape
    n //= parts
    g = group_of(n, 8)
    first = part * (n // g)
    args = [d, top, bottom, slope, w]
    specs = [
        gen_spec(g, d.shape, first),
        gen_spec(g, top.shape, d.shape[0] // g + first),
        gen_spec(g, bottom.shape, d.shape[0] // g + first),
        whole_spec(slope.shape),
        whole_spec(w.shape),
    ]
    aliases = {}
    if out is not None:
        aliases = {len(args): 0}
        args.append(out)
        specs.append(pl.BlockSpec(memory_space=pl.ANY))
    return pl.pallas_call(
        backward_kernel,
        grid=(n // g,),
        in_specs=specs,
        out_specs=gen_spec(g, d.shape, first),
        out_shape=jax.ShapeDtypeStruct(d.shape, BF16),
        input_output_aliases=aliases,
        cost_estimate=cost(n, band, width, c),
        name="backward",
    )(*args)


def list_call(kernel, place, chan, extra, extra_specs, out_shape, out_spec, name, step):
    count = place.shape[1]
    row = lambda: pl.BlockSpec((1, step), lambda i: (0, i))
    return pl.pallas_call(
        kernel,
        grid=(count // step,),
        in_specs=[row(), row()] + extra_specs,
        out_specs=out_spec,
        out_shape=out_shape,
        cost_estimate=pl.CostEstimate(
            flops=count * 256 * 512, bytes_accessed=count * 12, transcendentals=0
        ),
        name=name,
    )(place, chan, extra)


def spread_values(place, chan, values, places, c):
    step = group_of(place.shape[1], 2048)
    return list_call(
        spread_kernel, place, chan, values,
        [pl.BlockSpec((1, step), lambda i: (0, i))],
        jax.ShapeDtypeStruct((places, c), F32),
        whole_spec((places, c)), "spread", step,
    )


def pick_values(place, chan, field):
    step = group_of(place.shape[1], 2048)
    high = field.astype(BF16)
    low = (field - high.astype(F32)).astype(BF16)
    split = jnp.concatenate([high, low], axis=1).T
    return list_call(
        pick_kernel, place, chan, split,
        [whole_spec(split.shape)],
        jax.ShapeDtypeStruct((1, place.shape[1]), F32),
        pl.BlockSpec((1, step), lambda i: (0, i)), "pick", step,
    )


def pair_weights(weight):
    c, o = weight.shape[2], weight.shape[3]
    zero = jnp.zeros((c, 3 * o), weight.dtype)
    side = jnp.transpose(weight, (0, 2, 1, 3)).reshape(3 * c, 3 * o)
    return jnp.concatenate(
        [
            jnp.concatenate([side, zero], axis=0),
            jnp.concatenate([zero, side], axis=0),
        ],
        axis=1,
    )


def conv_band(field, kernel):
    return lax.conv_general_dilated(
        field, kernel, (1, 1), ((0, 0), (1, 1)), dimension_numbers=DIMS,
        preferred_element_type=F32,
    )


def relu_terms(y_center, slope, products, radius, state, d_center, extra):
    unstable_mask = state == 2
    safe_r = jnp.where(unstable_mask, radius, 1.0)
    two_r = 2.0 * safe_r
    d_mu = d_center + extra
    d_lam = d_center * y_center + products
    d_yc = slope * d_center + jnp.where(unstable_mask, (d_lam - d_mu * y_center) / two_r, 0.0)
    d_rad = jnp.where(
        unstable_mask,
        -d_lam * y_center / (two_r * safe_r)
        + d_mu * (0.25 + y_center * y_center / (two_r * two_r)),
        0.0,
    )
    return d_yc, d_rad


def slope_of(y_center, radius, state):
    unstable_mask = state == 2
    safe_r = jnp.where(unstable_mask, radius, 1.0)
    return jnp.where(
        unstable_mask, (y_center + safe_r) / (2.0 * safe_r), jnp.where(state == 1, 1.0, 0.0)
    )


def on_device(center, gens, weight, bias, radius, state, unstable, d_center, d_gens, d_new):
    band, width, c = center.shape[1:]
    row_pos = lax.axis_index("rows")
    flipped = jnp.transpose(weight[::-1, ::-1], (0, 1, 3, 2))
    forward_w = pair_weights(weight)
    backward_w = pair_weights(flipped)
    x, d = gens[0], d_gens[0]

    def far(first_row, last_row, count):
        side = slice(0, count) if first_row == 0 else slice(band - count, band)
        one = slice(first_row, first_row + 1)
        return jnp.concatenate(
            [center[0, side].astype(F32), radius[0, one], state[0, one].astype(F32)], axis=0
        )

    low, high = neighbours(far(band - 1, band, 2), far(0, 1, 2), "rows")
    xd_top, xd_bottom = neighbours(
        *edge_rows(x, d), "rows"
    )
    n = x.shape[0]

    ids = unstable
    place = ids // c - row_pos * (band * width)
    chan = ids % c
    extra = spread_values(place, chan, d_new, band * width, c).reshape(band, width, c)

    wider = jnp.concatenate([low[:2].astype(BF16), center[0], high[:2].astype(BF16)], axis=0)
    padded = wider[1:-1][None]
    y_wide = conv_band(wider[None], weight)[0] + bias
    y_center = y_wide[1:-1]
    radius_wide = jnp.concatenate([low[2:3], radius[0], high[2:3]], axis=0)
    state_wide = jnp.concatenate([low[3:], state[0].astype(F32), high[3:]], axis=0)
    slopes = slope_of(y_wide, radius_wide, state_wide)
    slope = slopes[1:-1]

    spare_unit = lax.axis_size("gen") * lax.axis_size("rows") * lax.axis_size("img") * 8
    spare = -(9 * c) % spare_unit or spare_unit
    partial_sum = products_call(x, xd_top, xd_bottom, d, forward_w)
    grads = Filler(
        lambda slope_in, acc, part, parts: wgrad_call(
            x, xd_top, xd_bottom, d, slope_in, acc, part, parts, 9 * c + spare
        ),
        slope, 2, (1, 2),
    )
    products = sum_over(partial_sum, "gen", [grads, grads])
    local = grads.finish()

    d_yc, d_rad = relu_terms(
        y_center, slope, products, radius[0], state[0], d_center[0], extra
    )
    d_yc16 = d_yc.astype(BF16)
    t_top, t_bottom = edges(d_yc16, "rows")
    d_padded = jnp.concatenate([t_top, d_yc16, t_bottom], axis=0)[None]
    grad_center = conv_band(d_padded, flipped).astype(BF16)

    wide = jnp.pad(padded[0], ((0, 0), (1, 1), (0, 0)))
    windows = jnp.concatenate(
        [
            wide[a : a + band, b : b + width].reshape(-1, c)
            for a in range(3)
            for b in range(3)
        ],
        axis=1,
    )
    center_w = lax.dot_general(
        windows, d_yc16.reshape(-1, c), (((0,), (0,)), ((), ())), preferred_element_type=F32
    )
    center_b = jnp.sum(d_yc, axis=(0, 1))[None]
    late = jnp.concatenate([center_w, center_b, jnp.zeros((spare - 1, c), F32)], axis=0)
    fill = Filler(
        lambda slopes_in, out, part, parts: backward_call(
            d, xd_top, xd_bottom, slopes_in, backward_w, out, part, parts
        ),
        slopes, 4 if n % 32 == 0 else 1, (2, 3, 4, 5),
    )
    totals = total_over_mesh(local, late, fill)
    out = fill.finish()
    positions = float(band * lax.axis_size("rows") * width * lax.axis_size("img"))
    grad_weight = (totals[: 9 * c] / positions).reshape(3, 3, c, c)
    grad_bias = totals[9 * c] / positions

    picked = pick_values(place, chan, d_rad.reshape(-1, c))
    block = unstable.shape[1] // lax.axis_size("rows")
    mine = scatter_sum(picked.reshape(-1, 128) if block % 128 == 0 else picked[0], "rows")
    grad_radius = mine.reshape(1, block)
    return (grad_center, out[None], grad_weight, grad_bias, grad_radius)


def solution(mesh):
    return jax.shard_map(
        on_device,
        mesh=mesh,
        in_specs=(
            P("img", "rows", None, None),
            P("img", "gen", "rows", None, None),
            P(),
            P(),
            P("img", "rows", None, None),
            P("img", "rows", None, None),
            P("img", None),
            P("img", "rows", None, None),
            P("img", "gen", "rows", None, None),
            P("img", None),
        ),
        out_specs=(
            P("img", "rows", None, None),
            P("img", "gen", "rows", None, None),
            P(),
            P(),
            P("img", "rows"),
        ),
        check_vma=False,
    )
```

```python
import functools

import jax
import jax.numpy as jnp
from jax import lax
from jax.experimental import pallas as pl
from jax.experimental.pallas import tpu as pltpu
from jax.sharding import PartitionSpec as P


DIMS = ("NHWC", "HWIO", "NHWC")
F32 = jnp.float32
BF16 = jnp.bfloat16


def neighbours(last, first, axis):
    n = lax.axis_size(axis)
    up = [(i, i + 1) for i in range(n - 1)]
    down = [(i + 1, i) for i in range(n - 1)]
    return lax.ppermute(last, axis, up), lax.ppermute(first, axis, down)


def edges(array, axis):
    return neighbours(array[-1:], array[:1], axis)


class Filler:
    def __init__(self, call, operand, pieces, steps):
        self.call, self.operand, self.pieces = call, operand, pieces
        self.steps, self.step, self.done, self.out = steps, 0, 0, None

    def run(self, operand):
        self.out = self.call(operand, self.out, self.done, self.pieces)
        self.done += 1

    def __call__(self, got, before):
        self.step += 1
        if self.step in self.steps and self.done < self.pieces:
            _, operand = lax.optimization_barrier((before, self.operand))
            self.run(operand)
            got, self.out = lax.optimization_barrier((got, self.out))
        return got

    def finish(self):
        while self.done < self.pieces:
            self.run(self.operand)
        return self.out


def power_of_two(n):
    return n & (n - 1) == 0


def sum_over(value, axis, fills):
    n = lax.axis_size(axis)
    if not power_of_two(n):
        return lax.psum(value, axis)
    bit = 1
    while bit < n:
        got = lax.ppermute(value, axis, [(i, i ^ bit) for i in range(n)])
        if fills:
            got = fills.pop(0)(got, value)
        value = value + got
        bit *= 2
    return value


def block_of(array, index, size):
    return lax.dynamic_slice_in_dim(array, index * size, size, 0)


def scatter_sum(chunk, axis):
    n, me = lax.axis_size(axis), lax.axis_index(axis)
    if not power_of_two(n):
        return lax.psum_scatter(chunk, axis, scatter_dimension=0, tiled=True)
    bit = n // 2
    while bit >= 1:
        half = chunk.shape[0] // 2
        mine = (me // bit) % 2
        part = block_of(chunk, 1 - mine, half)
        got = lax.ppermute(part, axis, [(i, i ^ bit) for i in range(n)])
        chunk = block_of(chunk, mine, half) + got
        bit //= 2
    return chunk


def halve(chunk, late, axis, fill):
    n, me = lax.axis_size(axis), lax.axis_index(axis)
    bit = 1
    while bit < n:
        half = chunk.shape[0] // 2
        mine = (me // bit) % 2
        part = block_of(chunk, 1 - mine, half)
        got = lax.ppermute(part, axis, [(i, i ^ bit) for i in range(n)])
        got = fill(got, part)
        chunk = block_of(chunk, mine, half) + got
        if late is not None:
            late = block_of(late, mine, half)
        bit *= 2
    return chunk, late


def double(chunk, axis, fill):
    n, me = lax.axis_size(axis), lax.axis_index(axis)
    bit = n // 2
    while bit >= 1:
        mine = (me // bit) % 2
        got = lax.ppermute(chunk, axis, [(i, i ^ bit) for i in range(n)])
        got = fill(got, chunk)
        low = jnp.where(mine == 0, chunk, got)
        high = jnp.where(mine == 0, got, chunk)
        chunk = jnp.concatenate([low, high], axis=0)
        bit //= 2
    return chunk


def total_over_mesh(local, late, fill):
    sizes = [lax.axis_size(a) for a in ("gen", "img", "rows")]
    if not all(power_of_two(s) for s in sizes):
        return lax.psum(lax.psum(local, "gen") + late, ("rows", "img"))
    chunk, late = halve(local, late, "gen", fill)
    chunk = chunk + late
    chunk, _ = halve(chunk, None, "img", fill)
    chunk = sum_over(chunk, "rows", [fill] * lax.axis_size("rows"))
    return double(double(chunk, "img", fill), "gen", fill)


def row_pairs(rows):
    pairs = (len(rows) - 2) // 2
    c = rows[0].shape[-1]
    flat = [r.reshape(-1, c) for r in rows]
    return jnp.concatenate(
        [jnp.concatenate([flat[2 * p + i] for i in range(4)], axis=1) for p in range(pairs)],
        axis=0,
    )


def band_rows(x_ref, top_ref, bottom_ref):
    band = x_ref.shape[1]
    return [top_ref[...]] + [x_ref[:, h] for h in range(band)] + [bottom_ref[...]]


def column(count, width):
    return lax.broadcasted_iota(jnp.int32, (count, 1), 0) % width


def to_right(v, col):
    return jnp.where(col == 0, 0.0, pltpu.roll(v, 1, 0))


def to_left(v, col, width):
    return jnp.where(col == width - 1, 0.0, pltpu.roll(v, v.shape[0] - 1, 0))


def conv_pairs(lhs, w_ref, r, width, c, col):
    span = 3 * c
    taps = jnp.dot(lhs, w_ref[:, r * span : (r + 1) * span], preferred_element_type=F32)
    return (
        to_right(taps[:, :c], col)
        + taps[:, c : 2 * c]
        + to_left(taps[:, 2 * c :], col, width)
    )


def products_kernel(x_ref, top_ref, bottom_ref, d_ref, w_ref, out_ref):
    @pl.when(pl.program_id(0) == 0)
    def _():
        out_ref[...] = jnp.zeros_like(out_ref)

    g, band, width, c = x_ref.shape
    lhs = row_pairs(band_rows(x_ref, top_ref, bottom_ref))
    col = column(lhs.shape[0], width)
    for r in range(2):
        y = conv_pairs(lhs, w_ref, r, width, c, col).reshape(band // 2, g, width, c)
        for p in range(band // 2):
            h = 2 * p + r
            out_ref[h] += jnp.sum(d_ref[:, h].astype(F32) * y[p], axis=0)


def wgrad_kernel(last, x_ref, top_ref, bottom_ref, d_ref, slope_ref, *refs):
    acc_ref = refs[-1]

    @pl.when(pl.program_id(0) == 0)
    def _():
        acc_ref[...] = refs[0][...] if len(refs) == 3 else jnp.zeros_like(acc_ref)

    _, band, width, c = x_ref.shape
    lhs = row_pairs(band_rows(x_ref, top_ref, bottom_ref))
    col = column(lhs.shape[0], width)
    parts = []
    for r in range(2):
        d = jnp.concatenate(
            [
                (slope_ref[h][None] * d_ref[:, h].astype(F32)).reshape(-1, c)
                for h in range(r, band, 2)
            ],
            axis=0,
        )
        parts += [
            to_left(d, col, width).astype(BF16),
            d.astype(BF16),
            to_right(d, col).astype(BF16),
        ]
    rhs = jnp.concatenate(parts, axis=1)
    acc_ref[...] += lax.dot_general(
        lhs, rhs, (((0,), (0,)), ((), ())), preferred_element_type=F32
    )

    @pl.when(pl.program_id(0) == pl.num_programs(0) - 1)
    def _():
        out_ref = refs[-2]
        if not last:
            out_ref[...] = acc_ref[...]
            return
        for a in range(3):
            for b in range(3):
                first = acc_ref[a * c : (a + 1) * c, b * c : (b + 1) * c]
                second = acc_ref[(a + 1) * c : (a + 2) * c, (3 + b) * c : (4 + b) * c]
                out_ref[(a * 3 + b) * c : (a * 3 + b + 1) * c] = first + second
        spare = out_ref.shape[0] - 9 * c
        out_ref[9 * c :] = jnp.zeros((spare, c), F32)


def backward_kernel(d_ref, top_ref, bottom_ref, slope_ref, w_ref, *refs):
    out_ref = refs[-1]
    g, band, width, c = d_ref.shape
    rows = [
        (slope_ref[j][None] * row.astype(F32)).astype(BF16)
        for j, row in enumerate(band_rows(d_ref, top_ref, bottom_ref))
    ]
    lhs = row_pairs(rows)
    col = column(lhs.shape[0], width)
    for r in range(2):
        y = conv_pairs(lhs, w_ref, r, width, c, col).reshape(band // 2, g, width, c)
        for p in range(band // 2):
            out_ref[:, 2 * p + r] = y[p].astype(BF16)


def spread_kernel(place_ref, chan_ref, value_ref, out_ref):
    @pl.when(pl.program_id(0) == 0)
    def _():
        out_ref[...] = jnp.zeros_like(out_ref)

    places, c = out_ref.shape
    count = place_ref.shape[1]
    at_place = lax.broadcasted_iota(jnp.int32, (places, count), 0) == place_ref[...]
    at_chan = lax.broadcasted_iota(jnp.int32, (c, count), 0) == chan_ref[...]
    value = value_ref[...]
    high = value.astype(BF16).astype(F32)
    low = value - high
    terms = jnp.concatenate(
        [jnp.where(at_chan, part, 0.0).astype(BF16) for part in (high, low)], axis=0
    )
    hit = jnp.where(at_place, 1.0, 0.0).astype(BF16)
    both = lax.dot_general(hit, terms, (((1,), (1,)), ((), ())), preferred_element_type=F32)
    out_ref[...] += both[:, :c] + both[:, c:]


def pick_kernel(place_ref, chan_ref, field_ref, out_ref):
    places = field_ref.shape[1]
    c = field_ref.shape[0] // 2
    count = place_ref.shape[1]
    at_place = lax.broadcasted_iota(jnp.int32, (places, count), 0) == place_ref[...]
    at_chan = lax.broadcasted_iota(jnp.int32, (c, count), 0) == chan_ref[...]
    hit = jnp.where(at_place, 1.0, 0.0).astype(BF16)
    got = jnp.dot(field_ref[...], hit, preferred_element_type=F32)
    got = got[:c] + got[c:]
    out_ref[...] = jnp.sum(jnp.where(at_chan, got, 0.0), axis=0, keepdims=True)


def group_of(count, most):
    g = min(count, most)
    while count % g:
        g -= 1
    return g


def gen_spec(g, shape, first=0):
    zeros = (0,) * (len(shape) - 1)
    return pl.BlockSpec((g,) + tuple(shape[1:]), lambda i: (i + first,) + zeros)


def whole_spec(shape):
    zeros = (0,) * len(shape)
    return pl.BlockSpec(tuple(shape), lambda i: zeros)


def cost(count, band, width, c):
    return pl.CostEstimate(
        flops=count * band * width * c * c * 24,
        bytes_accessed=count * band * width * c * 4,
        transcendentals=0,
    )


def edges_kernel(x_last, d_last, x_first, d_first, last_ref, first_ref):
    n = x_last.shape[0]
    last_ref[:n] = x_last[:, 0]
    last_ref[n:] = d_last[:, 0]
    first_ref[:n] = x_first[:, 0]
    first_ref[n:] = d_first[:, 0]


def edge_rows(x, d):
    n, band, width, c = x.shape
    row = lambda h: pl.BlockSpec((n, 1, width, c), lambda i: (0, h, 0, 0))
    shape = (2 * n, width, c)
    return pl.pallas_call(
        edges_kernel,
        grid=(1,),
        in_specs=[row(band - 1), row(band - 1), row(0), row(0)],
        out_specs=[whole_spec(shape)] * 2,
        out_shape=[jax.ShapeDtypeStruct(shape, BF16)] * 2,
        name="edges",
    )(x, d, x, d)


def products_call(x, top, bottom, d, w):
    n, band, width, c = x.shape
    g = group_of(n, 8)
    return pl.pallas_call(
        products_kernel,
        grid=(n // g,),
        in_specs=[
            gen_spec(g, x.shape),
            gen_spec(g, top.shape),
            gen_spec(g, bottom.shape),
            gen_spec(g, d.shape),
            whole_spec(w.shape),
        ],
        out_specs=whole_spec((band, width, c)),
        out_shape=jax.ShapeDtypeStruct((band, width, c), F32),
        cost_estimate=cost(n, band, width, c),
        name="products",
    )(x, top, bottom, d, w)


def wgrad_call(x, top, bottom, d, slope, acc, part, parts, rows):
    n, band, width, c = x.shape
    n //= parts
    g = group_of(n, 16)
    first = part * (n // g)
    last = part == parts - 1
    shape = (rows, c) if last else (4 * c, 6 * c)
    args = [x, top, bottom, d, slope] + ([] if acc is None else [acc])
    return pl.pallas_call(
        functools.partial(wgrad_kernel, last),
        grid=(n // g,),
        in_specs=[
            gen_spec(g, x.shape, first),
            gen_spec(g, top.shape, first),
            gen_spec(g, bottom.shape, first),
            gen_spec(g, d.shape, first),
        ]
        + [whole_spec(a.shape) for a in args[4:]],
        out_specs=whole_spec(shape),
        out_shape=jax.ShapeDtypeStruct(shape, F32),
        scratch_shapes=[pltpu.VMEM((4 * c, 6 * c), F32)],
        cost_estimate=cost(n, band, width, c),
        name="wgrad",
    )(*args)


def backward_call(d, top, bottom, slope, w, out, part, parts):
    n, band, width, c = d.shape
    n //= parts
    g = group_of(n, 8)
    first = part * (n // g)
    args = [d, top, bottom, slope, w]
    specs = [
        gen_spec(g, d.shape, first),
        gen_spec(g, top.shape, d.shape[0] // g + first),
        gen_spec(g, bottom.shape, d.shape[0] // g + first),
        whole_spec(slope.shape),
        whole_spec(w.shape),
    ]
    aliases = {}
    if out is not None:
        aliases = {len(args): 0}
        args.append(out)
        specs.append(pl.BlockSpec(memory_space=pl.ANY))
    return pl.pallas_call(
        backward_kernel,
        grid=(n // g,),
        in_specs=specs,
        out_specs=gen_spec(g, d.shape, first),
        out_shape=jax.ShapeDtypeStruct(d.shape, BF16),
        input_output_aliases=aliases,
        cost_estimate=cost(n, band, width, c),
        name="backward",
    )(*args)


def list_call(kernel, place, chan, extra, extra_specs, out_shape, out_spec, step):
    count = place.shape[1]
    row = lambda: pl.BlockSpec((1, step), lambda i: (0, i))
    return pl.pallas_call(
        kernel,
        grid=(count // step,),
        in_specs=[row(), row()] + extra_specs,
        out_specs=out_spec,
        out_shape=out_shape,
        cost_estimate=pl.CostEstimate(
            flops=count * 256 * 512, bytes_accessed=count * 12, transcendentals=0
        ),
    )(place, chan, extra)


def spread_values(place, chan, values, places, c):
    step = group_of(place.shape[1], 2048)
    return list_call(
        spread_kernel, place, chan, values,
        [pl.BlockSpec((1, step), lambda i: (0, i))],
        jax.ShapeDtypeStruct((places, c), F32),
        whole_spec((places, c)), step,
    )


def pick_values(place, chan, field):
    step = group_of(place.shape[1], 2048)
    high = field.astype(BF16)
    low = (field - high.astype(F32)).astype(BF16)
    split = jnp.concatenate([high, low], axis=1).T
    return list_call(
        pick_kernel, place, chan, split,
        [whole_spec(split.shape)],
        jax.ShapeDtypeStruct((1, place.shape[1]), F32),
        pl.BlockSpec((1, step), lambda i: (0, i)), step,
    )


def pair_weights(weight):
    c, o = weight.shape[2], weight.shape[3]
    zero = jnp.zeros((c, 3 * o), weight.dtype)
    side = jnp.transpose(weight, (0, 2, 1, 3)).reshape(3 * c, 3 * o)
    return jnp.concatenate(
        [
            jnp.concatenate([side, zero], axis=0),
            jnp.concatenate([zero, side], axis=0),
        ],
        axis=1,
    )


def conv_band(field, kernel):
    return lax.conv_general_dilated(
        field, kernel, (1, 1), ((0, 0), (1, 1)), dimension_numbers=DIMS,
        preferred_element_type=F32,
    )


def relu_terms(y_center, slope, products, radius, state, d_center, extra):
    unstable_mask = state == 2
    safe_r = jnp.where(unstable_mask, radius, 1.0)
    two_r = 2.0 * safe_r
    d_mu = d_center + extra
    d_lam = d_center * y_center + products
    d_yc = slope * d_center + jnp.where(unstable_mask, (d_lam - d_mu * y_center) / two_r, 0.0)
    d_rad = jnp.where(
        unstable_mask,
        -d_lam * y_center / (two_r * safe_r)
        + d_mu * (0.25 + y_center * y_center / (two_r * two_r)),
        0.0,
    )
    return d_yc, d_rad


def slope_of(y_center, radius, state):
    unstable_mask = state == 2
    safe_r = jnp.where(unstable_mask, radius, 1.0)
    return jnp.where(
        unstable_mask, (y_center + safe_r) / (2.0 * safe_r), jnp.where(state == 1, 1.0, 0.0)
    )


def step(center, gens, weight, bias, radius, state, unstable, d_center, d_gens, d_new):
    band, width, c = center.shape[1:]
    row_pos = lax.axis_index("rows")
    flipped = jnp.transpose(weight[::-1, ::-1], (0, 1, 3, 2))
    forward_w = pair_weights(weight)
    backward_w = pair_weights(flipped)
    x, d = gens[0], d_gens[0]

    def far(first_row, count):
        side = slice(0, count) if first_row == 0 else slice(band - count, band)
        one = slice(first_row, first_row + 1)
        return jnp.concatenate(
            [center[0, side].astype(F32), radius[0, one], state[0, one].astype(F32)], axis=0
        )

    low, high = neighbours(far(band - 1, 2), far(0, 2), "rows")
    xd_top, xd_bottom = neighbours(*edge_rows(x, d), "rows")
    n = x.shape[0]

    ids = unstable
    place = ids // c - row_pos * (band * width)
    chan = ids % c
    extra = spread_values(place, chan, d_new, band * width, c).reshape(band, width, c)

    wider = jnp.concatenate([low[:2].astype(BF16), center[0], high[:2].astype(BF16)], axis=0)
    padded = wider[1:-1][None]
    y_wide = conv_band(wider[None], weight)[0] + bias
    y_center = y_wide[1:-1]
    radius_wide = jnp.concatenate([low[2:3], radius[0], high[2:3]], axis=0)
    state_wide = jnp.concatenate([low[3:], state[0].astype(F32), high[3:]], axis=0)
    slopes = slope_of(y_wide, radius_wide, state_wide)
    slope = slopes[1:-1]

    spare_unit = lax.axis_size("gen") * lax.axis_size("rows") * lax.axis_size("img") * 8
    spare = -(9 * c) % spare_unit or spare_unit
    partial_sum = products_call(x, xd_top, xd_bottom, d, forward_w)
    grads = Filler(
        lambda slope_in, acc, part, parts: wgrad_call(
            x, xd_top, xd_bottom, d, slope_in, acc, part, parts, 9 * c + spare
        ),
        slope, 2, (1, 2),
    )
    products = sum_over(partial_sum, "gen", [grads, grads])
    local = grads.finish()

    d_yc, d_rad = relu_terms(
        y_center, slope, products, radius[0], state[0], d_center[0], extra
    )
    d_yc16 = d_yc.astype(BF16)
    t_top, t_bottom = edges(d_yc16, "rows")
    d_padded = jnp.concatenate([t_top, d_yc16, t_bottom], axis=0)[None]
    grad_center = conv_band(d_padded, flipped).astype(BF16)

    wide = jnp.pad(padded[0], ((0, 0), (1, 1), (0, 0)))
    windows = jnp.concatenate(
        [
            wide[a : a + band, b : b + width].reshape(-1, c)
            for a in range(3)
            for b in range(3)
        ],
        axis=1,
    )
    center_w = lax.dot_general(
        windows, d_yc16.reshape(-1, c), (((0,), (0,)), ((), ())), preferred_element_type=F32
    )
    center_b = jnp.sum(d_yc, axis=(0, 1))[None]
    late = jnp.concatenate([center_w, center_b, jnp.zeros((spare - 1, c), F32)], axis=0)
    fill = Filler(
        lambda slopes_in, out, part, parts: backward_call(
            d, xd_top, xd_bottom, slopes_in, backward_w, out, part, parts
        ),
        slopes, 4 if n % 32 == 0 else 1, (3, 4, 5, 7),
    )
    totals = total_over_mesh(local, late, fill)
    out = fill.finish()
    positions = float(band * lax.axis_size("rows") * width * lax.axis_size("img"))
    grad_weight = (totals[: 9 * c] / positions).reshape(3, 3, c, c)
    grad_bias = totals[9 * c] / positions

    picked = pick_values(place, chan, d_rad.reshape(-1, c))
    block = unstable.shape[1] // lax.axis_size("rows")
    mine = scatter_sum(picked.reshape(-1, 128) if block % 128 == 0 else picked[0], "rows")
    grad_radius = mine.reshape(1, block)
    return (grad_center, out[None], grad_weight, grad_bias, grad_radius)


def solution(mesh):
    return jax.shard_map(
        step,
        mesh=mesh,
        in_specs=(
            P("img", "rows", None, None),
            P("img", "gen", "rows", None, None),
            P(),
            P(),
            P("img", "rows", None, None),
            P("img", "rows", None, None),
            P("img", None),
            P("img", "rows", None, None),
            P("img", "gen", "rows", None, None),
            P("img", None),
        ),
        out_specs=(
            P("img", "rows", None, None),
            P("img", "gen", "rows", None, None),
            P(),
            P(),
            P("img", "rows"),
        ),
        check_vma=False,
    )
```
